32 devices in a mesh: group: 2 (over y), ctx: 4 (over z), head: 2 (over x), pool: 2 (over core).
Axes of the slice: x: 2, y: 2, z: 4, core: 2. Of those that a mesh axis runs over, the one named last changes fastest.
Arguments:
- queries: bfloat16 [1024, 8192], P(('group', 'ctx'), ('head', 'pool')), parts along dimension 0, may hold values from -100 to 100
- new_kv: bfloat16 [2, 1024, 1024], P(None, ('group', 'ctx'), ('head', 'pool')), parts along dimension 1, may hold values from -5 to 5
- pool: bfloat16 [2, 64, 128, 1024], P(None, ('group', 'ctx'), None, ('head', 'pool')), parts along dimension 1, may hold values from -4.5 to 4.5
- block_table: int32 [64], P('group'), parts along dimension 0, may hold values from 0 to 31, as said below
- span_order: int32 [8], P('group'), parts along dimension 0, may hold values from 0 to 3, each once
Outputs:
- attended: bfloat16 [1024, 8192], P(('group', 'ctx'), ('head', 'pool')), parts along dimension 0
The draws below stay inside these ranges and needn't reach their ends.
There are 2 independent parts, one for each index of `group`. The reference program is written for one: setup_inputs(seed, part) draws one part's arguments, and reference() takes and returns one part's arrays. A program takes and returns all parts, laid end to end along the dimension named above; each array names one. Nothing has to cross between parts.
Inputs may be any that keep to these rules, and one draw needn't show every extreme that they name: `block_table`: all ids differ. Index h of ctx holds pool ids h * 8 to (h + 1) * 8 - 1. In each aligned group of 8 entries (entries k * 8 to (k + 1) * 8 - 1), every index of ctx holds either none or exactly 2 of the ids.
All inputs are finite; a program needn't handle non-finite values.
Results may differ from the reference program's by a relative error of at most 0.0045.
Values may be sent and summed in bfloat16 or wider, within the bound.
No kernel may reach another device: no remote copies, remote signals or barrier semaphores. Data moves between devices by JAX's collectives and lax.ppermute only.
A program may use at most 128 MiB of HBM per device.

```python
import math
import jax
import jax.numpy as jnp
from jax import lax

HD = 128
QH = 64
KVH = 8
BLK = 128
CAP = 2
Q_DEV = 128
PB_DEV = 8
POOL_DEV = 8
NEW = 512
PREFIX_BLOCKS = 32
PREFIX = 4096
POOL_BLOCKS = 32
N_CTX = 4


def draw_pair(key):
    query_key = jax.random.fold_in(key, 101)
    keys_key = jax.random.fold_in(key, 202)
    values_key = jax.random.fold_in(key, 303)
    base_query = jnp.clip(jax.random.normal(query_key, (NEW, QH, HD), jnp.float32), -4.0, 4.0)
    key_rows = jnp.clip(jax.random.normal(keys_key, (NEW, KVH, HD), jnp.float32), -4.4, 4.4)
    value_rows = jnp.clip(jax.random.normal(values_key, (NEW, KVH, HD), jnp.float32), -4.4, 4.4)
    query_rows = 2.5 * base_query
    stacked = jnp.stack([key_rows, value_rows]).reshape(2, NEW, KVH * HD)
    return (query_rows.reshape(NEW, QH * HD), stacked)


def draw_queries(key, part):
    return draw_pair(key)[0].astype(jnp.bfloat16)


def draw_new_kv(key, part):
    return draw_pair(key)[1].astype(jnp.bfloat16)


def draw_block_table(key, part):
    per_owner = PB_DEV // CAP
    hot_bias = jax.random.randint(jax.random.fold_in(key, 7), (N_CTX,), 0, 4) * 256
    noise_score = jax.random.randint(jax.random.fold_in(key, 8), (N_CTX, N_CTX), 0, 256)
    holder_score = (noise_score + hot_bias[None, :]) * N_CTX + jnp.arange(N_CTX, dtype=jnp.int32)[None, :]
    chosen = lax.top_k(holder_score, per_owner)[1].astype(jnp.int32)
    holders = jnp.repeat(chosen, CAP, axis=1)
    within = jnp.tile(jnp.arange(CAP, dtype=jnp.int32), per_owner)
    rotation = jax.random.randint(jax.random.fold_in(key, 9), (N_CTX,), 0, POOL_DEV)
    owners = jnp.arange(N_CTX, dtype=jnp.int32)[:, None]
    pool_slot = (owners * CAP + within[None, :] + rotation[holders]) % POOL_DEV
    block_ids = holders * POOL_DEV + pool_slot
    shuffle_score = jax.random.randint(jax.random.fold_in(key, 10), (N_CTX, PB_DEV), 0, 4096) * PB_DEV + jnp.arange(PB_DEV, dtype=jnp.int32)[None, :]
    shuffle = jnp.argsort(shuffle_score, axis=1, stable=True)
    block_ids = jnp.take_along_axis(block_ids, shuffle, axis=1)
    return block_ids.reshape(-1).astype(jnp.int32)


def block_levels(stream_key, shape, shards, least, top_value):
    factor_of, own = 1.0, jax.random.fold_in(stream_key, 6)
    for axis_at, blocks in shards:
        steps = jnp.exp(jax.random.uniform(jax.random.fold_in(own, axis_at), (blocks,), jnp.float32, least / len(shards), top_value / len(shards)))
        factor_of = factor_of * jnp.repeat(steps, shape[axis_at] // blocks).reshape([-1 if axis == axis_at else 1 for axis in range(len(shape))])
    return factor_of


def scatter_about(stream_key, dims, scale, limit, pieces=(), kind=jnp.bfloat16):
    result = jax.random.normal(stream_key, dims, jnp.float32) * scale
    if len(pieces) > 0:
        result = block_levels(stream_key, dims, pieces, -0.22, 0.18) * result
    return jnp.clip(result, min=-limit, max=limit).astype(kind)


def setup_inputs(seed: int = 0, part: int = 0) -> dict:
    key_of = jax.random.split(jax.random.key(seed), 6)
    part_splits = jax.random.split(jax.random.fold_in(key_of[5], part), 6)
    queries = draw_queries(jax.random.fold_in(jax.random.fold_in(key_of[5], part), 71), part)
    new_kv = draw_new_kv(jax.random.fold_in(jax.random.fold_in(key_of[5], part), 71), part)
    pool = scatter_about(part_splits[2], (2, POOL_BLOCKS, BLK, KVH * HD), 1.0, 4.5, ((1, 4), (3, 4)))
    block_table = draw_block_table(jax.random.fold_in(jax.random.fold_in(key_of[5], part), 71), part)
    span_order = jax.random.permutation(part_splits[4], N_CTX).astype(jnp.int32)
    return {"queries": queries, "new_kv": new_kv, "pool": pool, "block_table": block_table, "span_order": span_order}


masked_score = -1e+30

def reference(queries, new_kv, pool, block_table, span_order):
    blocks = jnp.take(pool, block_table, axis=1)
    prefix_kv = blocks.reshape(2, PREFIX_BLOCKS * BLK, KVH * HD)
    context = jnp.concatenate([prefix_kv, new_kv], axis=1)
    new_index = jnp.arange(NEW, dtype=jnp.int32)
    query_pos = PREFIX + span_order[new_index // Q_DEV] * Q_DEV + new_index % Q_DEV
    key_pos = jnp.concatenate([jnp.arange(PREFIX, dtype=jnp.int32), query_pos.astype(jnp.int32)])
    allowed = key_pos[None, :] <= query_pos[:, None]
    query_heads = queries.reshape(NEW, QH, HD)
    key_heads = context[0].reshape(PREFIX + NEW, KVH, HD)
    value_heads = context[1].reshape(PREFIX + NEW, KVH, HD)
    per_group = QH // KVH
    score_scale = 1.0 / math.sqrt(HD)

    def one_head(head_index):
        query_head = lax.dynamic_index_in_dim(query_heads, head_index, 1, keepdims=False)
        key_head = lax.dynamic_index_in_dim(key_heads, head_index // per_group, 1, keepdims=False)
        value_head = lax.dynamic_index_in_dim(value_heads, head_index // per_group, 1, keepdims=False)
        scores = jnp.dot(query_head, key_head.T, preferred_element_type=jnp.float32) * score_scale
        scores = jnp.where(allowed, scores, masked_score)
        row_max = lax.optimization_barrier(jnp.max(scores, axis=1, keepdims=True))
        exp_scores = jnp.where(allowed, jnp.exp(scores - row_max), 0.0)
        row_total = lax.optimization_barrier(jnp.sum(exp_scores, axis=1, keepdims=True))
        weighted = jnp.dot(exp_scores.astype(jnp.bfloat16), value_head, preferred_element_type=jnp.float32)
        return weighted / row_total
    per_head = lax.map(one_head, jnp.arange(QH, dtype=jnp.int32))
    return per_head.transpose(1, 0, 2).reshape(NEW, QH * HD).astype(jnp.bfloat16)
```

```python
import functools
import math

import jax
import jax.numpy as jnp
from jax import lax
from jax.experimental import pallas as pl
from jax.experimental.pallas import tpu as pltpu
from jax.sharding import PartitionSpec as P

HD = 128
QH = 64
KVH = 8
CAP = 2
LANES = 128

masked_score = -1e30
exponent_scale = math.log2(math.e) / math.sqrt(HD)


def redistribute(pool, block_table, cycle_size, my_index):
    pool_dev = pool.shape[1]
    block_len = pool.shape[2]
    blocks_dev = block_table.shape[0] // cycle_size
    owner_table = block_table.reshape(cycle_size, blocks_dev)
    holder = owner_table // pool_dev
    local_id = owner_table - holder * pool_dev
    same_holder = holder[:, :, None] == holder[:, None, :]
    earlier = (
        jnp.arange(blocks_dev, dtype=jnp.int32)[:, None]
        < jnp.arange(blocks_dev, dtype=jnp.int32)[None, :]
    )
    rank_in_list = jnp.sum((same_holder & earlier[None, :, :]).astype(jnp.int32), axis=1)
    slot_match = (holder[:, None, :] == my_index) & (
        rank_in_list[:, None, :] == jnp.arange(CAP, dtype=jnp.int32)[None, :, None]
    )
    source = jnp.sum(jnp.where(slot_match, local_id[:, None, :], 0), axis=2)
    filled = jnp.any(slot_match, axis=2)
    picked = jnp.take(pool, source.reshape(-1), axis=1)
    picked = jnp.where(filled.reshape(1, -1, 1, 1), picked, jnp.zeros_like(picked))
    outgoing = picked.reshape(2, cycle_size, CAP, block_len, pool.shape[3])
    incoming = lax.all_to_all(outgoing, "ctx", split_axis=1, concat_axis=1, tiled=True)
    my_holder = lax.dynamic_index_in_dim(holder, my_index, 0, keepdims=False)
    my_rank = lax.dynamic_index_in_dim(rank_in_list, my_index, 0, keepdims=False)
    flat_slot = my_holder * CAP + my_rank
    arrived = incoming.reshape(2, cycle_size * CAP, block_len, pool.shape[3])
    return jnp.take(arrived, flat_slot, axis=1)


def attend_kernel(per_group, new_rows, kv_count, has_state, packed, where_ref, span_ref, *refs):
    refs = list(refs)
    q_ref = refs.pop(0)
    kv_refs = [refs.pop(0) for _ in range(kv_count)]
    if has_state:
        state_o, state_lse = refs.pop(0), refs.pop(0)
        lse_in = state_lse[...]
    if packed:
        (out_ref,) = refs
    else:
        out_ref, out_lse = refs
    rows = q_ref.shape[0]
    query_base = span_ref[where_ref[0]] * rows
    lane = lax.broadcasted_iota(jnp.int32, (rows, LANES), 1)
    ahead = lax.broadcasted_iota(jnp.int32, (rows, new_rows), 1) - lax.broadcasted_iota(
        jnp.int32, (rows, new_rows), 0
    )
    keys, values, masks = [], [], []
    for at, kv_ref in enumerate(kv_refs):
        key_base = span_ref[where_ref[1 + at]] * new_rows
        masks.append(ahead <= query_base - key_base)
        keys.append(kv_ref[0])
        value = kv_ref[1]
        values.append(jnp.concatenate([value, jnp.ones_like(value)], axis=1))
    stats = jnp.zeros((rows, LANES), jnp.float32)
    for g in range(per_group):
        query = q_ref[:, g * HD : (g + 1) * HD]
        pieces = []
        if has_state:
            pieces.append((state_o[:, g * HD : (g + 1) * HD], lse_in[:, g : g + 1], None))
        for key, value, mask in zip(keys, values, masks):
            scores = lax.dot_general(
                query, key, (((1,), (1,)), ((), ())), preferred_element_type=jnp.float32
            )
            edge = scores.shape[1] - new_rows
            scores = jnp.concatenate(
                [scores[:, :edge], jnp.where(mask, scores[:, edge:], masked_score)], axis=1
            )
            top = jnp.max(scores, axis=1, keepdims=True)
            weights = jnp.exp2((scores - top) * exponent_scale)
            both = jnp.dot(weights.astype(jnp.bfloat16), value, preferred_element_type=jnp.float32)
            pieces.append((both[:, :HD], top * exponent_scale, both[:, HD:]))
        peak = functools.reduce(jnp.maximum, [piece[1] for piece in pieces])
        total_out, total = 0.0, 0.0
        for out, level, weight in pieces:
            factor = jnp.exp2(level - peak) if len(pieces) > 1 else 1.0
            total_out = total_out + out * factor
            total = total + (factor if weight is None else weight * factor)
        total = jnp.broadcast_to(total, total_out.shape)
        normal = total_out / total
        stats = jnp.where(lane == g, peak + jnp.log2(total), stats)
        if packed:
            out_ref[g * rows : (g + 1) * rows, :] = normal.astype(jnp.bfloat16)
        else:
            out_ref[:, g * HD : (g + 1) * HD] = normal
    if packed:
        for at in range(rows // LANES):
            level = stats[at * LANES : (at + 1) * LANES, :].T[:per_group, :]
            high = level.astype(jnp.bfloat16).astype(jnp.float32)
            middle = (level - high).astype(jnp.bfloat16).astype(jnp.float32)
            low = level - high - middle
            terms = jnp.concatenate([high, middle, low, jnp.zeros_like(low)], axis=0)
            start = per_group * rows + at * 4 * per_group
            out_ref[start : start + 4 * per_group, :] = terms.astype(jnp.bfloat16)
    else:
        out_lse[...] = stats


def whole(array):
    return pl.BlockSpec(array.shape, lambda i: (0,) * array.ndim)


def attend(name, queries, column, per_group, new_rows, kvs, where, spans, state=None, packed=False):
    rows = queries.shape[0]
    width = per_group * HD
    in_specs = [pl.BlockSpec(memory_space=pltpu.SMEM)] * 2
    in_specs.append(pl.BlockSpec((rows, width), lambda i: (0, column)))
    in_specs += [whole(kv) for kv in kvs]
    args = [where, spans, queries, *kvs]
    if state is not None:
        in_specs += [whole(part) for part in state]
        args += list(state)
    if packed:
        packed_rows = per_group * rows + 4 * per_group * (rows // LANES)
        out_shape = [jax.ShapeDtypeStruct((packed_rows, HD), jnp.bfloat16)]
    else:
        out_shape = [
            jax.ShapeDtypeStruct((rows, width), jnp.float32),
            jax.ShapeDtypeStruct((rows, LANES), jnp.float32),
        ]
    key_rows = sum(kv.shape[1] for kv in kvs)
    score_count = rows * per_group * key_rows
    result = pl.pallas_call(
        functools.partial(
            attend_kernel, per_group, new_rows, len(kvs), state is not None, packed
        ),
        grid=(1,),
        in_specs=in_specs,
        out_specs=[whole(shape) for shape in out_shape],
        out_shape=out_shape,
        name=name,
        cost_estimate=pl.CostEstimate(
            flops=4 * score_count * HD,
            bytes_accessed=2 * rows * width * 4 + 4 * key_rows * HD,
            transcendentals=score_count,
        ),
    )(*args)
    return result[0] if packed else tuple(result)


def finish_kernel(per_group, count, *refs):
    state_o, state_lse = refs[0], refs[1]
    packs = refs[2 : 2 + count]
    out_ref = refs[-1]
    rows = state_o.shape[0]
    lse = state_lse[...]
    tables = []
    for pack in packs:
        parts = []
        for at in range(rows // LANES):
            start = per_group * rows + at * 4 * per_group
            terms = pack[start : start + 4 * per_group, :].astype(jnp.float32)
            level = (
                terms[:per_group]
                + terms[per_group : 2 * per_group]
                + terms[2 * per_group : 3 * per_group]
            )
            level = jnp.concatenate(
                [level, jnp.zeros((LANES - per_group, LANES), jnp.float32)], axis=0
            )
            parts.append(level.T)
        tables.append(jnp.concatenate(parts, axis=0) if len(parts) > 1 else parts[0])
    for g in range(per_group):
        outs = [state_o[:, g * HD : (g + 1) * HD]]
        levels = [lse[:, g : g + 1]]
        for pack, table in zip(packs, tables):
            outs.append(pack[g * rows : (g + 1) * rows, :].astype(jnp.float32))
            levels.append(table[:, g : g + 1])
        peak = functools.reduce(jnp.maximum, levels)
        factors = [jnp.exp2(level - peak) for level in levels]
        inverse = 1.0 / functools.reduce(jnp.add, factors)
        mixed = functools.reduce(
            jnp.add, [out * (factor * inverse) for out, factor in zip(outs, factors)]
        )
        out_ref[:, g * HD : (g + 1) * HD] = mixed.astype(jnp.bfloat16)


def finish(name, state, packs, per_group, column, columns, earlier):
    rows = state[0].shape[0]
    width = per_group * HD
    args = [*state, *packs]
    in_specs = [whole(arg) for arg in args]
    aliases = {}
    if earlier is not None:
        aliases = {len(args): 0}
        args.append(earlier)
        in_specs.append(pl.BlockSpec(memory_space=pl.ANY))
    return pl.pallas_call(
        functools.partial(finish_kernel, per_group, len(packs)),
        grid=(1,),
        in_specs=in_specs,
        out_specs=pl.BlockSpec((rows, width), lambda i: (0, column)),
        out_shape=jax.ShapeDtypeStruct((rows, columns * width), jnp.bfloat16),
        input_output_aliases=aliases,
        name=name,
        cost_estimate=pl.CostEstimate(
            flops=6 * rows * width, bytes_accessed=8 * rows * width, transcendentals=0
        ),
    )(*args)


def local(queries, new_kv, pool, block_table, span_order):
    cycle_size = lax.axis_size("ctx")
    my_index = lax.axis_index("ctx")
    per_group = QH // KVH
    kv_heads = new_kv.shape[2] // HD
    new_rows = new_kv.shape[1]
    width = per_group * HD
    if block_table.shape[0] == cycle_size * pool.shape[1]:
        prefix = pool
    else:
        prefix = redistribute(pool, block_table, cycle_size, my_index)
    prefix = prefix.reshape(2, -1, pool.shape[3])

    members = 2 if cycle_size % 2 == 0 else 1
    teams = cycle_size // members

    def target(index, step):
        team, member = index // members, index % members
        return ((team + step) % teams) * members + (members - 1 - member)

    my_team, my_member = my_index // members, my_index % members
    pair_index = my_team * members + (members - 1 - my_member)

    own, near, visitors = [], [], {}
    for h in range(kv_heads):
        columns = slice(h * HD, (h + 1) * HD)
        own.append(jnp.concatenate([prefix[:, :, columns], new_kv[:, :, columns]], axis=1))
    for h in range(kv_heads):
        if members > 1:
            swap = [(i, target(i, 0)) for i in range(cycle_size)]
            near.append(lax.ppermute(own[h], "ctx", swap))
        for step in range(1, teams):
            out = [(i, target(i, step)) for i in range(cycle_size)]
            visitors[h, step] = lax.ppermute(
                queries[:, h * width : (h + 1) * width], "ctx", out
            )

    mine = jnp.stack([my_index, my_index]).astype(jnp.int32)
    mine_near = jnp.stack([my_index, pair_index]).astype(jnp.int32)
    result = None
    states = [
        attend(f"own{h}", queries, h, per_group, new_rows, [own[h]], mine, span_order)
        for h in range(kv_heads)
    ]
    for h in range(kv_heads):
        packs = []
        for step in range(1, teams):
            guest_index = ((my_team + teams - step) % teams) * members + (members - 1 - my_member)
            kvs = [own[h]] + near[h : h + 1]
            where = jnp.stack([guest_index, my_index, pair_index]).astype(jnp.int32)
            part = attend(
                f"guest{h}_{step}",
                visitors[h, step],
                0,
                per_group,
                new_rows,
                kvs,
                where,
                span_order,
                packed=True,
            )
            back = [(target(i, step), i) for i in range(cycle_size)]
            packs.append(lax.ppermute(part, "ctx", back))
        state = states[h]
        if members > 1:
            state = attend(
                f"near{h}",
                queries,
                h,
                per_group,
                new_rows,
                [near[h]],
                mine_near,
                span_order,
                state=state,
            )
        result = finish(f"finish{h}", state, packs, per_group, h, kv_heads, result)
    return result


def solution(mesh):
    return jax.shard_map(
        local,
        mesh=mesh,
        in_specs=(
            P(("group", "ctx"), ("head", "pool")),
            P(None, ("group", "ctx"), ("head", "pool")),
            P(None, ("group", "ctx"), None, ("head", "pool")),
            P("group"),
            P("group"),
        ),
        out_specs=P(("group", "ctx"), ("head", "pool")),
        check_vma=False,
    )
```
